32 devices in a mesh: rows: 8 (over z, y), cols: 4 (over x, core).
Axes of the slice: x: 2, y: 2, z: 4, core: 2. Of those that a mesh axis runs over, the one named last changes fastest.
Arguments:
- depth: float32 [128, 16384], P('rows', 'cols'), may hold values from 0.08 to 6.3, as said below
- hit_mask: int32 [128, 16384], P('rows', 'cols'), may hold values 0 or 1
- hit_count: int32 [128, 16384], P('rows', 'cols'), may hold values from 1 to 8
- grad_h: float32 [128, 16384], P('rows', 'cols'), may hold values from -6 to 6
- grad_v: float32 [128, 16384], P('rows', 'cols'), may hold values from -6 to 6
Outputs:
- solution_field: float32 [128, 16384], P('rows', 'cols')
- residual: float32 [128, 16384], P('rows', 'cols')
The draws below stay inside these ranges and needn't reach their ends.
Inputs may be any that keep to these rules, and one draw needn't show every extreme that they name: `depth`: positive depths.
All inputs are finite; a program needn't handle non-finite values. No bound on the sum of `hit_mask` on one device may be relied on, other than what follows from the above.
Results may differ from the reference program's by a relative error of at most 0.0003.
Values sent between devices are 32-bit elements; how exact they have to be, the bound alone decides.
A program may use at most 64 MiB of HBM per device.

```python
import math
import jax
import jax.numpy as jnp
from jax import lax

ITERS = 12
NR = 128
NC = 16384


def draw_depth(key, part):
    row = lax.broadcasted_iota(jnp.float32, (NR, NC), 0)
    column = lax.broadcasted_iota(jnp.float32, (NR, NC), 1)
    ramp = 0.3 * jnp.exp(math.log(10.0) * (0.5 * row / NR + 0.5 * column / NC))
    rough = jnp.exp(jax.random.uniform(key, (NR, NC), jnp.float32, -0.7, 0.7))
    return ramp * rough


def touch_ends(values, own_key, least, largest):
    longest = values.shape.index(max(values.shape))
    spots = []
    for shift in (0, 1):
        where = [jax.random.randint(jax.random.fold_in(own_key, axis), (), 0, length) for axis, length in enumerate(values.shape)]
        where[longest] = (where[longest] + shift) % values.shape[longest]
        spots.append(tuple(where))
    return values.at[spots[0]].set(least).at[spots[1]].set(largest)


def level_of(stream_key, dims, shards, low, top_value):
    factor_of, own = 1.0, jax.random.fold_in(stream_key, 6)
    for position, shards_of in shards:
        heights = jnp.exp(jax.random.uniform(jax.random.fold_in(own, position), (shards_of,), jnp.float32, low / len(shards), top_value / len(shards)))
        factor_of = factor_of * jnp.repeat(heights, dims[position] // shards_of).reshape([-1 if axis == position else 1 for axis in range(len(dims))])
    return factor_of


def noise(own_key, dims, width, bound, shards=(), held_as=jnp.bfloat16):
    level = level_of(own_key, dims, shards, -0.22, 0.18) if shards else 1.0
    result = jax.random.normal(own_key, dims, jnp.float32) * width * level
    return jnp.minimum(jnp.maximum(result, -bound), bound).astype(held_as)


def setup_inputs(seed: int = 0) -> dict:
    arg_keys = jax.random.split(jax.random.key(seed), 6)
    depth = draw_depth(jax.random.fold_in(arg_keys[5], 71), 0)
    hit_mask = touch_ends((jax.random.randint(arg_keys[1], (NR, NC), 0, 4) < 1).astype(jnp.int32), jax.random.fold_in(arg_keys[1], 1), 0, 1)
    hit_count = touch_ends(jax.random.randint(arg_keys[2], (NR, NC), 1, 9), jax.random.fold_in(arg_keys[2], 1), 1, 8).astype(jnp.int32)
    grad_h = noise(arg_keys[3], (NR, NC), 1.0, 6.0, ((0, 8), (1, 4)), jnp.float32)
    grad_v = noise(arg_keys[4], (NR, NC), 1.0, 6.0, ((0, 8), (1, 4)), jnp.float32)
    return dict(depth=depth, hit_mask=hit_mask, hit_count=hit_count, grad_h=grad_h, grad_v=grad_v)


prior_weight = 0.1
smooth_weight = 2.0


def build(depth, hit_mask, hit_count, grad_h, grad_v):
    column = lax.broadcasted_iota(jnp.int32, depth.shape, 1)
    row = lax.broadcasted_iota(jnp.int32, depth.shape, 0)
    east = jnp.where(column + 1 < NC, jnp.exp(-0.5 * grad_h * grad_h), 0.0)
    south = jnp.where(row + 1 < NR, jnp.exp(-0.5 * grad_v * grad_v), 0.0)
    west = jnp.pad(east, ((0, 0), (1, 0)))[:, :-1]
    north = jnp.pad(south, ((1, 0), (0, 0)))[:-1, :]
    confidence = (hit_mask * hit_count).astype(jnp.float32) + prior_weight
    center = confidence + smooth_weight * (east + west + south + north)
    return (center, east, west, south, north), confidence * depth


def operate(field, coefficients):
    center, east, west, south, north = coefficients
    padded = jnp.pad(field, 1)
    beside = east * padded[1:-1, 2:] + west * padded[1:-1, :-2] + south * padded[2:, 1:-1] + north * padded[:-2, 1:-1]
    return center * field - smooth_weight * beside


def reference(depth, hit_mask, hit_count, grad_h, grad_v):
    coefficients, right_side = build(depth, hit_mask, hit_count, grad_h, grad_v)
    solution_field = jnp.zeros_like(right_side)
    residual = right_side
    direction = right_side
    norm_now = jnp.sum(residual * residual)
    for iteration in range(ITERS):
        image = operate(direction, coefficients)
        alpha = norm_now / jnp.sum(direction * image)
        solution_field = solution_field + alpha * direction
        residual = residual - alpha * image
        norm_next = jnp.sum(residual * residual)
        direction = residual + (norm_next / norm_now) * direction
        norm_now = norm_next
    return solution_field, residual
```

```python
import functools

import jax
import jax.numpy as jnp
from jax import lax
from jax.experimental import pallas as pl
from jax.experimental.pallas import tpu as pltpu
from jax.sharding import PartitionSpec as P

ITERS = 12

prior_weight = 0.1
smooth_weight = 2.0
LANES = 128
MESH = pl.DeviceIdType.MESH


def each(start, stop, body):
    if stop - start <= 8:
        for k in range(start, stop):
            body(k)
    else:
        lax.fori_loop(start, stop, lambda k, c: (body(k), c)[1], 0)


def kernel(
    nr, nc,
    depth, hit_mask, hit_count, grad_h, grad_v,
    x, r,
    conf, east, south, w, z, s, p, n,
    e_left, s_above, e_send, s_send,
    left, right, above, below, first_tile, last_tile, top, bottom,
    by_col, by_row,
    coef_send, coef_recv, halo_send, halo_recv, col_send, col_recv, row_send, row_recv,
):
    me_r = lax.axis_index("rows")
    me_c = lax.axis_index("cols")
    rows, cols = depth.shape
    tiles = cols // LANES
    has_above, has_below = me_r > 0, me_r < nr - 1
    has_left, has_right = me_c > 0, me_c < nc - 1

    def row_peer(k):
        return (lax.rem(me_r + k, nr), me_c)

    def col_peer(k):
        return (me_r, lax.rem(me_c + k, nc))

    barrier = pltpu.get_barrier_semaphore()
    each(1, nr, lambda k: pl.semaphore_signal(barrier, inc=1, device_id=row_peer(k), device_id_type=MESH))
    each(1, nc, lambda k: pl.semaphore_signal(barrier, inc=1, device_id=col_peer(k), device_id_type=MESH))

    row_id = lax.broadcasted_iota(jnp.int32, (rows, LANES), 0)
    lane_id = lax.broadcasted_iota(jnp.int32, (rows, LANES), 1)

    def at(j):
        return slice(j * LANES, (j + 1) * LANES)

    for j in range(tiles):
        c = at(j)
        confidence = (hit_mask[:, c] * hit_count[:, c]).astype(jnp.float32) + prior_weight
        h, v = grad_h[:, c], grad_v[:, c]
        e = smooth_weight * jnp.exp(-0.5 * h * h)
        if j == tiles - 1:
            e = jnp.where(jnp.logical_and(lane_id == LANES - 1, jnp.logical_not(has_right)), 0.0, e)
        so = smooth_weight * jnp.exp(-0.5 * v * v)
        so = jnp.where(jnp.logical_and(row_id == rows - 1, jnp.logical_not(has_below)), 0.0, so)
        b = confidence * depth[:, c]
        zero = jnp.zeros((rows, LANES), jnp.float32)
        conf[:, c] = confidence
        east[:, c] = e
        south[:, c] = so
        r[:, c] = b
        x[:, c] = zero
        z[:, c] = zero
        s[:, c] = zero
        p[:, c] = zero
        s_send[:, c] = so[rows - 1 :, :]
        top[:, c] = b[:1, :]
        bottom[:, c] = b[rows - 1 :, :]
        if j == 0:
            first_tile[...] = b
        if j == tiles - 1:
            last_tile[...] = b
            e_send[...] = e

    @pl.when(jnp.logical_not(has_above))
    def _():
        s_above[...] = jnp.zeros_like(s_above)
        above[...] = jnp.zeros_like(above)

    @pl.when(jnp.logical_not(has_below))
    def _():
        below[...] = jnp.zeros_like(below)

    @pl.when(jnp.logical_not(has_left))
    def _():
        e_left[...] = jnp.zeros_like(e_left)
        left[...] = jnp.zeros_like(left)

    @pl.when(jnp.logical_not(has_right))
    def _():
        right[...] = jnp.zeros_like(right)

    pl.semaphore_wait(barrier, nr - 1 + nc - 1)

    up, down = (me_r - 1, me_c), (me_r + 1, me_c)
    lefthand, righthand = (me_r, me_c - 1), (me_r, me_c + 1)

    def remote(src, dst, send, recv, to):
        return pltpu.make_async_remote_copy(
            src_ref=src, dst_ref=dst, send_sem=send, recv_sem=recv, device_id=to, device_id_type=MESH
        )

    def halo_copies(slot):
        return (
            (remote(top, below.at[slot], halo_send.at[0], halo_recv.at[slot, 0], up), has_above, has_below),
            (remote(bottom, above.at[slot], halo_send.at[1], halo_recv.at[slot, 1], down), has_below, has_above),
            (remote(first_tile, right.at[slot], halo_send.at[2], halo_recv.at[slot, 2], lefthand), has_left, has_right),
            (remote(last_tile, left.at[slot], halo_send.at[3], halo_recv.at[slot, 3], righthand), has_right, has_left),
        )

    def coef_copies():
        return (
            (remote(s_send, s_above, coef_send.at[0], coef_recv.at[0], down), has_below, has_above),
            (remote(e_send, e_left, coef_send.at[1], coef_recv.at[1], righthand), has_right, has_left),
        )

    def start(copies):
        for copy, sends, _ in copies:
            pl.when(sends)(copy.start)

    def wait_recv(copies):
        for copy, _, receives in copies:
            pl.when(receives)(copy.wait_recv)

    def wait_send(copies):
        for copy, sends, _ in copies:
            pl.when(sends)(copy.wait_send)

    def stencil(src, slot, emit):
        def to_left(v):
            return pltpu.roll(v, LANES - 1, 1)

        def to_right(v):
            return pltpu.roll(v, 1, 1)

        v = src[:, at(0)]
        moved = to_left(v)
        before = left[slot]
        flow = e_left[...] * (before - jnp.where(lane_id < LANES - 1, to_left(before), moved))
        carried = to_right(flow)
        for j in range(tiles):
            c = at(j)
            following = src[:, at(j + 1)] if j + 1 < tiles else right[slot]
            moved_next = to_left(following)
            flow = east[:, c] * (v - jnp.where(lane_id < LANES - 1, moved, moved_next))
            shifted = to_right(flow)
            from_left = jnp.where(lane_id > 0, shifted, carried)
            lower = jnp.where(row_id < rows - 1, pltpu.roll(v, rows - 1, 0), below[slot, :, c])
            fall = south[:, c] * (v - lower)
            upper = s_above[:, c] * (above[slot, :, c] - v)
            from_above = jnp.where(row_id > 0, pltpu.roll(fall, 1, 0), upper)
            emit(c, v, conf[:, c] * v + ((flow - from_left) + (fall - from_above)))
            v, moved, carried = following, moved_next, shifted

    def folded(acc):
        return jnp.sum(acc, axis=0, keepdims=True)

    first, coefs = halo_copies(0), coef_copies()
    start(first)
    start(coefs)
    wait_recv(first)
    wait_recv(coefs)
    wait_send(first)
    wait_send(coefs)
    acc = [jnp.zeros((rows, LANES), jnp.float32)] * 2

    def keep_edges(c, value):
        top[:, c] = value[:1, :]
        bottom[:, c] = value[rows - 1 :, :]
        if c.start == 0:
            first_tile[...] = value
        if c.stop == cols:
            last_tile[...] = value

    def begin(c, v, image):
        w[:, c] = image
        keep_edges(c, image)
        acc[0] = acc[0] + v * v
        acc[1] = acc[1] + v * image

    stencil(r, 0, begin)

    def reduce_cols(slot, rr, rw):
        by_col[slot, me_c, 0:1, :] = folded(rr)
        by_col[slot, me_c, 1:2, :] = folded(rw)

        def copy(k, source):
            return remote(by_col.at[slot, me_c], by_col.at[slot, me_c], col_send.at[k], col_recv.at[slot, source], col_peer(k))

        each(1, nc, lambda k: copy(k, me_c).start())

        def finish():
            def arrival(k):
                source = lax.rem(me_c + k, nc)
                here = by_col.at[slot, source]
                remote(here, here, col_send.at[k], col_recv.at[slot, source], col_peer(k)).wait_recv()

            each(1, nc, arrival)
            each(1, nc, lambda k: copy(k, me_c).wait_send())
            total = by_col[slot, 0]
            for k in range(1, nc):
                total = total + by_col[slot, k]
            return total

        return finish

    def reduce_rows(slot, part):
        by_row[slot, me_r] = part

        def copy(k):
            return remote(by_row.at[slot, me_r], by_row.at[slot, me_r], row_send.at[k], row_recv.at[slot, me_r], row_peer(k))

        each(1, nr, lambda k: copy(k).start())

        def finish():
            def arrival(k):
                source = lax.rem(me_r + k, nr)
                here = by_row.at[slot, source]
                remote(here, here, row_send.at[k], row_recv.at[slot, source], row_peer(k)).wait_recv()

            each(1, nr, arrival)
            each(1, nr, lambda k: copy(k).wait_send())
            if nr <= 8:
                total = by_row[slot, 0]
                for k in range(1, nr):
                    total = total + by_row[slot, k]
            else:
                total = lax.fori_loop(1, nr, lambda k, t: t + by_row[slot, k], by_row[slot, 0])
            total = jnp.sum(total, axis=1, keepdims=True)
            return total[0:1], total[1:2]

        return finish

    def wide(scalar):
        return jnp.broadcast_to(scalar, (rows, LANES))

    def iteration(i, state, last=False):
        rr, rw, gamma_old, alpha_old = state
        slot = lax.rem(i + 1, 2)
        halos = () if last else halo_copies(slot)
        finish_cols = reduce_cols(slot, rr, rw)
        start(halos)
        finish_rows = reduce_rows(slot, finish_cols())
        wait_recv(halos)

        def keep(c, v, image):
            n[:, c] = image

        if not last:
            stencil(w, slot, keep)
        wait_send(halos)
        gamma, delta = finish_rows()
        beta = gamma / gamma_old
        beta = jnp.where(i == 0, jnp.zeros_like(beta), beta)
        alpha = gamma / (delta - beta * gamma / alpha_old)
        a, b = wide(alpha), wide(beta)
        rr = jnp.zeros((rows, LANES), jnp.float32)
        rw = rr
        for j in range(tiles):
            c = at(j)
            shadow = w[:, c] + b * s[:, c]
            direction = r[:, c] + b * p[:, c]
            x[:, c] = x[:, c] + a * direction
            residual = r[:, c] - a * shadow
            r[:, c] = residual
            if not last:
                images = n[:, c] + b * z[:, c]
                watched = w[:, c] - a * images
                s[:, c] = shadow
                p[:, c] = direction
                z[:, c] = images
                w[:, c] = watched
                keep_edges(c, watched)
                rr = rr + residual * residual
                rw = rw + residual * watched
        return rr, rw, gamma, alpha

    unity = jnp.ones((1, 1), jnp.float32)
    state = lax.fori_loop(0, ITERS - 1, iteration, (acc[0], acc[1], unity, unity))
    iteration(ITERS - 1, state, last=True)


def solution(mesh):
    nr, nc = mesh.shape["rows"], mesh.shape["cols"]

    def on_device(*inputs):
        rows, cols = inputs[0].shape
        block = jax.ShapeDtypeStruct((rows, cols), jnp.float32)

        def held(*shape):
            return pltpu.VMEM(shape, jnp.float32)

        dma = pltpu.SemaphoreType.DMA
        return pl.pallas_call(
            functools.partial(kernel, nr, nc),
            out_shape=(block, block),
            in_specs=[pl.BlockSpec(memory_space=pltpu.VMEM)] * 5,
            out_specs=[pl.BlockSpec(memory_space=pltpu.VMEM)] * 2,
            scratch_shapes=[held(rows, cols)] * 8
            + [held(rows, LANES), held(1, cols), held(rows, LANES), held(1, cols)]
            + [held(2, rows, LANES), held(2, rows, LANES), held(2, 1, cols), held(2, 1, cols)]
            + [held(rows, LANES), held(rows, LANES), held(1, cols), held(1, cols)]
            + [held(2, nc, 2, LANES), held(2, nr, 2, LANES)]
            + [dma((2,)), dma((2,)), dma((4,)), dma((2, 4)), dma((nc,)), dma((2, nc)), dma((nr,)), dma((2, nr))],
            compiler_params=pltpu.CompilerParams(collective_id=0, has_side_effects=True),
        )(*inputs)

    spec = P("rows", "cols")
    return jax.shard_map(
        on_device, mesh=mesh, in_specs=(spec,) * 5, out_specs=(spec, spec), check_vma=False
    )
```

```python
import functools

import jax
import jax.numpy as jnp
from jax import lax
from jax.experimental import pallas as pl
from jax.experimental.pallas import tpu as pltpu
from jax.sharding import PartitionSpec as P

ITERS = 12

prior_weight = 0.1
smooth_weight = 2.0
LANES = 128
DOTS = 10
MESH = pl.DeviceIdType.MESH


def each(start, stop, body):
    if stop - start <= 8:
        for k in range(start, stop):
            body(k)
    else:
        lax.fori_loop(start, stop, lambda k, c: (body(k), c)[1], 0)


def kernel(
    nr, nc,
    depth, hit_mask, hit_count, grad_h, grad_v,
    x, r0,
    conf, east, south, r1, r2, r3, q0, q1, q2, old2,
    e_left, s_above, e_send, s_send,
    left, right, above, below, first_tile, last_tile, top, bottom,
    by_col, by_row,
    coef_send, coef_recv, halo_send, halo_recv, col_send, col_recv, row_send, row_recv,
):
    me_r = lax.axis_index("rows")
    me_c = lax.axis_index("cols")
    rows, cols = depth.shape
    tiles = cols // LANES
    has_above, has_below = me_r > 0, me_r < nr - 1
    has_left, has_right = me_c > 0, me_c < nc - 1

    def row_peer(k):
        return (lax.rem(me_r + k, nr), me_c)

    def col_peer(k):
        return (me_r, lax.rem(me_c + k, nc))

    barrier = pltpu.get_barrier_semaphore()
    each(1, nr, lambda k: pl.semaphore_signal(barrier, inc=1, device_id=row_peer(k), device_id_type=MESH))
    each(1, nc, lambda k: pl.semaphore_signal(barrier, inc=1, device_id=col_peer(k), device_id_type=MESH))

    row_id = lax.broadcasted_iota(jnp.int32, (rows, LANES), 0)
    lane_id = lax.broadcasted_iota(jnp.int32, (rows, LANES), 1)

    def at(j):
        return slice(j * LANES, (j + 1) * LANES)

    for j in range(tiles):
        c = at(j)
        confidence = (hit_mask[:, c] * hit_count[:, c]).astype(jnp.float32) + prior_weight
        h, v = grad_h[:, c], grad_v[:, c]
        e = smooth_weight * jnp.exp(-0.5 * h * h)
        if j == tiles - 1:
            e = jnp.where(jnp.logical_and(lane_id == LANES - 1, jnp.logical_not(has_right)), 0.0, e)
        so = smooth_weight * jnp.exp(-0.5 * v * v)
        so = jnp.where(jnp.logical_and(row_id == rows - 1, jnp.logical_not(has_below)), 0.0, so)
        b = confidence * depth[:, c]
        zero = jnp.zeros((rows, LANES), jnp.float32)
        conf[:, c] = confidence
        east[:, c] = e
        south[:, c] = so
        r0[:, c] = b
        for held in (x, q0, q1, q2, old2):
            held[:, c] = zero
        s_send[:, c] = so[rows - 1 :, :]
        top[:, c] = b[:1, :]
        bottom[:, c] = b[rows - 1 :, :]
        if j == 0:
            first_tile[...] = b
        if j == tiles - 1:
            last_tile[...] = b
            e_send[...] = e

    @pl.when(jnp.logical_not(has_above))
    def _():
        s_above[...] = jnp.zeros_like(s_above)
        above[...] = jnp.zeros_like(above)

    @pl.when(jnp.logical_not(has_below))
    def _():
        below[...] = jnp.zeros_like(below)

    @pl.when(jnp.logical_not(has_left))
    def _():
        e_left[...] = jnp.zeros_like(e_left)
        left[...] = jnp.zeros_like(left)

    @pl.when(jnp.logical_not(has_right))
    def _():
        right[...] = jnp.zeros_like(right)

    pl.semaphore_wait(barrier, nr - 1 + nc - 1)

    up, down = (me_r - 1, me_c), (me_r + 1, me_c)
    lefthand, righthand = (me_r, me_c - 1), (me_r, me_c + 1)

    def remote(src, dst, send, recv, to):
        return pltpu.make_async_remote_copy(
            src_ref=src, dst_ref=dst, send_sem=send, recv_sem=recv, device_id=to, device_id_type=MESH
        )

    def halo_copies(slot):
        return (
            (remote(top, below.at[slot], halo_send.at[0], halo_recv.at[slot, 0], up), has_above, has_below),
            (remote(bottom, above.at[slot], halo_send.at[1], halo_recv.at[slot, 1], down), has_below, has_above),
            (remote(first_tile, right.at[slot], halo_send.at[2], halo_recv.at[slot, 2], lefthand), has_left, has_right),
            (remote(last_tile, left.at[slot], halo_send.at[3], halo_recv.at[slot, 3], righthand), has_right, has_left),
        )

    def coef_copies():
        return (
            (remote(s_send, s_above, coef_send.at[0], coef_recv.at[0], down), has_below, has_above),
            (remote(e_send, e_left, coef_send.at[1], coef_recv.at[1], righthand), has_right, has_left),
        )

    def start(copies):
        for copy, sends, _ in copies:
            pl.when(sends)(copy.start)

    def wait_recv(copies):
        for copy, _, receives in copies:
            pl.when(receives)(copy.wait_recv)

    def wait_send(copies):
        for copy, sends, _ in copies:
            pl.when(sends)(copy.wait_send)

    def stencil(src, slot, emit):
        def to_left(v):
            return pltpu.roll(v, LANES - 1, 1)

        def to_right(v):
            return pltpu.roll(v, 1, 1)

        v = src[:, at(0)]
        moved = to_left(v)
        before = left[slot]
        flow = e_left[...] * (before - jnp.where(lane_id < LANES - 1, to_left(before), moved))
        carried = to_right(flow)
        for j in range(tiles):
            c = at(j)
            following = src[:, at(j + 1)] if j + 1 < tiles else right[slot]
            moved_next = to_left(following)
            flow = east[:, c] * (v - jnp.where(lane_id < LANES - 1, moved, moved_next))
            shifted = to_right(flow)
            from_left = jnp.where(lane_id > 0, shifted, carried)
            lower = jnp.where(row_id < rows - 1, pltpu.roll(v, rows - 1, 0), below[slot, :, c])
            fall = south[:, c] * (v - lower)
            upper = s_above[:, c] * (above[slot, :, c] - v)
            from_above = jnp.where(row_id > 0, pltpu.roll(fall, 1, 0), upper)
            emit(c, v, conf[:, c] * v + ((flow - from_left) + (fall - from_above)))
            v, moved, carried = following, moved_next, shifted

    def folded(acc):
        return jnp.sum(acc, axis=0, keepdims=True)

    def folded(acc):
        return jnp.sum(acc, axis=0, keepdims=True)

    def keep_edges(c, value):
        top[:, c] = value[:1, :]
        bottom[:, c] = value[rows - 1 :, :]
        if c.start == 0:
            first_tile[...] = value
        if c.stop == cols:
            last_tile[...] = value

    def reduce_cols(slot, sums):
        for k in range(DOTS):
            by_col[slot, me_c, k : k + 1, :] = folded(sums[k])

        def copy(k, source):
            return remote(by_col.at[slot, me_c], by_col.at[slot, me_c], col_send.at[k], col_recv.at[slot, source], col_peer(k))

        each(1, nc, lambda k: copy(k, me_c).start())

        def finish():
            def arrival(k):
                source = lax.rem(me_c + k, nc)
                here = by_col.at[slot, source]
                remote(here, here, col_send.at[k], col_recv.at[slot, source], col_peer(k)).wait_recv()

            each(1, nc, arrival)
            each(1, nc, lambda k: copy(k, me_c).wait_send())
            total = by_col[slot, 0]
            for k in range(1, nc):
                total = total + by_col[slot, k]
            return total

        return finish

    def reduce_rows(slot, part):
        part = jnp.broadcast_to(jnp.sum(part, axis=1, keepdims=True), (DOTS, LANES))
        mine = lax.broadcasted_iota(jnp.int32, (DOTS, LANES), 0) == lax.broadcasted_iota(jnp.int32, (DOTS, LANES), 1)
        by_row[slot, me_r] = folded(jnp.where(mine, part, 0.0))

        def copy(k):
            return remote(by_row.at[slot, me_r], by_row.at[slot, me_r], row_send.at[k], row_recv.at[slot, me_r], row_peer(k))

        each(1, nr, lambda k: copy(k).start())

        def finish():
            def arrival(k):
                source = lax.rem(me_r + k, nr)
                here = by_row.at[slot, source]
                remote(here, here, row_send.at[k], row_recv.at[slot, source], row_peer(k)).wait_recv()

            each(1, nr, arrival)
            each(1, nr, lambda k: copy(k).wait_send())
            if nr <= 8:
                total = by_row[slot, 0]
                for k in range(1, nr):
                    total = total + by_row[slot, k]
            else:
                total = lax.fori_loop(1, nr, lambda k, t: t + by_row[slot, k], by_row[slot, 0])
            return [total[:, k : k + 1] for k in range(DOTS)]

        return finish

    def wide(scalar):
        return jnp.broadcast_to(scalar, (rows, LANES))

    def added(sums, pairs):
        return tuple(total + a * b for total, (a, b) in zip(sums, pairs))

    def stencil_into(dst, edges):
        def emit(c, v, image):
            dst[:, c] = image
            if edges:
                keep_edges(c, image)

        return emit

    def exchange(slot):
        halos = halo_copies(slot)
        start(halos)
        return halos

    def arrive(halos):
        wait_recv(halos)
        wait_send(halos)

    first, coefs = exchange(1), coef_copies()
    start(coefs)
    arrive(first)
    arrive(coefs)
    none = jnp.zeros((rows, LANES), jnp.float32)
    opening = [(none,) * 3]

    def begin(c, v, image):
        r1[:, c] = image
        keep_edges(c, image)
        opening[0] = added(opening[0], ((v, v), (v, image), (image, image)))

    stencil(r0, 1, begin)

    def block(i, state, last=False):
        sums, gamma_old, alpha_old = state
        slot = lax.rem(i, 2)
        arrive(exchange(0))
        cross = [(none,)]

        def second(c, v, image):
            r2[:, c] = image
            if not last:
                keep_edges(c, image)
            cross[0] = added(cross[0], ((v, image),))

        stencil(r1, 0, second)
        if not last:
            halos = exchange(1)
        finish_rows = reduce_rows(slot, reduce_cols(slot, sums + cross[0])())
        if not last:
            arrive(halos)
            stencil(r2, 1, stencil_into(r3, False))
        r0r0, r0r1, r1r1, r0q1, q0q1, r1q1, q1q1, r1q2, q1q2, r1r2 = finish_rows()
        beta = jnp.where(i == 0, jnp.zeros_like(r0r0), r0r0 / gamma_old)
        pap = r0r1 + beta * (2.0 * r0q1 + beta * q0q1)
        r0p1 = r0r1 + beta * r0q1
        p1p1 = r1r1 + beta * (2.0 * r1q1 + beta * q1q1)
        r1p1 = r1r1 + beta * r1q1
        p1p2 = r1r2 + beta * (2.0 * r1q2 + beta * q1q2)
        alpha = r0r0 / pap
        gamma = r0r0 - alpha * (2.0 * r0p1 - alpha * p1p1)
        beta_next = gamma / r0r0
        m0p1 = r0p1 - alpha * p1p1
        m0m1 = r0r1 - alpha * (2.0 * r1p1 - alpha * p1p2)
        alpha_next = gamma / (m0m1 + beta_next * (2.0 * m0p1 + beta_next * pap))
        b, a, b_, a_ = wide(beta), wide(alpha), wide(beta_next), wide(alpha_next)
        inverse = wide(1.0 / alpha_old)
        sums = (none,) * (DOTS - 1)
        for j in range(tiles):
            c = at(j)
            v0, v1, v2 = r0[:, c], r1[:, c], r2[:, c]
            p0 = v0 + b * q0[:, c]
            p1 = v1 + b * q1[:, c]
            p2 = v2 + b * q2[:, c]
            m0 = v0 - a * p1
            m1 = v1 - a * p2
            d0 = m0 + b_ * p0
            d1 = m1 + b_ * p1
            x[:, c] = x[:, c] + (a * p0 + a_ * d0)
            f0 = m0 - a_ * d1
            r0[:, c] = f0
            if not last:
                p3 = r3[:, c] + b * (inverse * (old2[:, c] - v2))
                m2 = v2 - a * p3
                d2 = m2 + b_ * p2
                f1 = m1 - a_ * d2
                r1[:, c] = f1
                q0[:, c] = d0
                q1[:, c] = d1
                q2[:, c] = d2
                old2[:, c] = m2
                keep_edges(c, f1)
                sums = added(
                    sums,
                    ((f0, f0), (f0, f1), (f1, f1), (f0, d1), (d0, d1), (f1, d1), (d1, d1), (f1, d2), (d1, d2)),
                )
        return sums, gamma, alpha_next

    unity = jnp.ones((1, 1), jnp.float32)
    state = (opening[0] + (none,) * (DOTS - 4), unity, unity)
    state = lax.fori_loop(0, ITERS // 2 - 1, block, state)
    block(ITERS // 2 - 1, state, last=True)


def solution(mesh):
    nr, nc = mesh.shape["rows"], mesh.shape["cols"]

    def on_device(*inputs):
        rows, cols = inputs[0].shape
        block = jax.ShapeDtypeStruct((rows, cols), jnp.float32)

        def held(*shape):
            return pltpu.VMEM(shape, jnp.float32)

        dma = pltpu.SemaphoreType.DMA
        return pl.pallas_call(
            functools.partial(kernel, nr, nc),
            out_shape=(block, block),
            in_specs=[pl.BlockSpec(memory_space=pltpu.VMEM)] * 5,
            out_specs=[pl.BlockSpec(memory_space=pltpu.VMEM)] * 2,
            scratch_shapes=[held(rows, cols)] * 10
            + [held(rows, LANES), held(1, cols), held(rows, LANES), held(1, cols)]
            + [held(2, rows, LANES), held(2, rows, LANES), held(2, 1, cols), held(2, 1, cols)]
            + [held(rows, LANES), held(rows, LANES), held(1, cols), held(1, cols)]
            + [held(2, nc, DOTS, LANES), held(2, nr, 1, LANES)]
            + [dma((2,)), dma((2,)), dma((4,)), dma((2, 4)), dma((nc,)), dma((2, nc)), dma((nr,)), dma((2, nr))],
            compiler_params=pltpu.CompilerParams(collective_id=0, has_side_effects=True),
        )(*inputs)

    spec = P("rows", "cols")
    return jax.shard_map(
        on_device, mesh=mesh, in_specs=(spec,) * 5, out_specs=(spec, spec), check_vma=False
    )
```

```python
import functools

import jax
import jax.numpy as jnp
from jax import lax
from jax.experimental import pallas as pl
from jax.experimental.pallas import tpu as pltpu
from jax.sharding import PartitionSpec as P

ITERS = 12

prior_weight = 0.1
smooth_weight = 2.0
LANES = 128
DOTS = 10
MESH = pl.DeviceIdType.MESH


def each(start, stop, body):
    if stop - start < 32:
        for k in range(start, stop):
            body(k)
    else:
        lax.fori_loop(start, stop, lambda k, c: (body(k), c)[1], 0)


def kernel(
    nr, nc,
    depth, hit_mask, hit_count, grad_h, grad_v,
    x, r0,
    conf, east, south, r1, r2, r3, q0, q1, q2, old2,
    e_left, s_above, e_send, s_send,
    left, right, above, below, first_tile, last_tile, top, bottom,
    folds, by_device,
    coef_send, coef_recv, halo_send, halo_recv, sum_send, sum_recv,
):
    me_r = lax.axis_index("rows")
    me_c = lax.axis_index("cols")
    rows, cols = depth.shape
    tiles = cols // LANES
    has_above, has_below = me_r > 0, me_r < nr - 1
    has_left, has_right = me_c > 0, me_c < nc - 1

    devices = nr * nc
    me = me_r * nc + me_c

    def peer(k):
        other = lax.rem(me + k, devices)
        return (other // nc, lax.rem(other, nc))

    barrier = pltpu.get_barrier_semaphore()
    each(1, devices, lambda k: pl.semaphore_signal(barrier, inc=1, device_id=peer(k), device_id_type=MESH))

    row_id = lax.broadcasted_iota(jnp.int32, (rows, LANES), 0)
    lane_id = lax.broadcasted_iota(jnp.int32, (rows, LANES), 1)

    def at(j):
        return slice(j * LANES, (j + 1) * LANES)

    for j in range(tiles):
        c = at(j)
        confidence = (hit_mask[:, c] * hit_count[:, c]).astype(jnp.float32) + prior_weight
        h, v = grad_h[:, c], grad_v[:, c]
        e = smooth_weight * jnp.exp(-0.5 * h * h)
        if j == tiles - 1:
            e = jnp.where(jnp.logical_and(lane_id == LANES - 1, jnp.logical_not(has_right)), 0.0, e)
        so = smooth_weight * jnp.exp(-0.5 * v * v)
        so = jnp.where(jnp.logical_and(row_id == rows - 1, jnp.logical_not(has_below)), 0.0, so)
        b = confidence * depth[:, c]
        zero = jnp.zeros((rows, LANES), jnp.float32)
        conf[:, c] = confidence
        east[:, c] = e
        south[:, c] = so
        r0[:, c] = b
        for held in (x, q0, q1, q2, old2):
            held[:, c] = zero
        s_send[:, c] = so[rows - 1 :, :]
        top[:, c] = b[:1, :]
        bottom[:, c] = b[rows - 1 :, :]
        if j == 0:
            first_tile[...] = b
        if j == tiles - 1:
            last_tile[...] = b
            e_send[...] = e

    @pl.when(jnp.logical_not(has_above))
    def _():
        s_above[...] = jnp.zeros_like(s_above)
        above[...] = jnp.zeros_like(above)

    @pl.when(jnp.logical_not(has_below))
    def _():
        below[...] = jnp.zeros_like(below)

    @pl.when(jnp.logical_not(has_left))
    def _():
        e_left[...] = jnp.zeros_like(e_left)
        left[...] = jnp.zeros_like(left)

    @pl.when(jnp.logical_not(has_right))
    def _():
        right[...] = jnp.zeros_like(right)

    pl.semaphore_wait(barrier, devices - 1)

    up, down = (me_r - 1, me_c), (me_r + 1, me_c)
    lefthand, righthand = (me_r, me_c - 1), (me_r, me_c + 1)

    def remote(src, dst, send, recv, to):
        return pltpu.make_async_remote_copy(
            src_ref=src, dst_ref=dst, send_sem=send, recv_sem=recv, device_id=to, device_id_type=MESH
        )

    def halo_copies(slot):
        return (
            (remote(top, below.at[slot], halo_send.at[0], halo_recv.at[slot, 0], up), has_above, has_below),
            (remote(bottom, above.at[slot], halo_send.at[1], halo_recv.at[slot, 1], down), has_below, has_above),
            (remote(first_tile, right.at[slot], halo_send.at[2], halo_recv.at[slot, 2], lefthand), has_left, has_right),
            (remote(last_tile, left.at[slot], halo_send.at[3], halo_recv.at[slot, 3], righthand), has_right, has_left),
        )

    def coef_copies():
        return (
            (remote(s_send, s_above, coef_send.at[0], coef_recv.at[0], down), has_below, has_above),
            (remote(e_send, e_left, coef_send.at[1], coef_recv.at[1], righthand), has_right, has_left),
        )

    def start(copies):
        for copy, sends, _ in copies:
            pl.when(sends)(copy.start)

    def wait_recv(copies):
        for copy, _, receives in copies:
            pl.when(receives)(copy.wait_recv)

    def wait_send(copies):
        for copy, sends, _ in copies:
            pl.when(sends)(copy.wait_send)

    def stencil(src, slot, emit):
        def to_left(v):
            return pltpu.roll(v, LANES - 1, 1)

        def to_right(v):
            return pltpu.roll(v, 1, 1)

        v = src[:, at(0)]
        moved = to_left(v)
        before = left[slot]
        flow = e_left[...] * (before - jnp.where(lane_id < LANES - 1, to_left(before), moved))
        carried = to_right(flow)
        for j in range(tiles):
            c = at(j)
            following = src[:, at(j + 1)] if j + 1 < tiles else right[slot]
            moved_next = to_left(following)
            flow = east[:, c] * (v - jnp.where(lane_id < LANES - 1, moved, moved_next))
            shifted = to_right(flow)
            from_left = jnp.where(lane_id > 0, shifted, carried)
            lower = jnp.where(row_id < rows - 1, pltpu.roll(v, rows - 1, 0), below[slot, :, c])
            fall = south[:, c] * (v - lower)
            upper = s_above[:, c] * (above[slot, :, c] - v)
            from_above = jnp.where(row_id > 0, pltpu.roll(fall, 1, 0), upper)
            emit(c, v, conf[:, c] * v + ((flow - from_left) + (fall - from_above)))
            v, moved, carried = following, moved_next, shifted

    def folded(acc):
        return jnp.sum(acc, axis=0, keepdims=True)

    def folded(acc):
        return jnp.sum(acc, axis=0, keepdims=True)

    def keep_edges(c, value):
        top[:, c] = value[:1, :]
        bottom[:, c] = value[rows - 1 :, :]
        if c.start == 0:
            first_tile[...] = value
        if c.stop == cols:
            last_tile[...] = value

    def reduce(slot, sums):
        for k in range(DOTS):
            folds[k : k + 1, :] = folded(sums[k])
        part = jnp.broadcast_to(jnp.sum(folds[...], axis=1, keepdims=True), (DOTS, LANES))
        mine = lax.broadcasted_iota(jnp.int32, (DOTS, LANES), 0) == lax.broadcasted_iota(jnp.int32, (DOTS, LANES), 1)
        by_device[slot, me] = folded(jnp.where(mine, part, 0.0))

        def copy(k):
            here = by_device.at[slot, me]
            return remote(here, here, sum_send.at[k], sum_recv.at[slot, me], peer(k))

        each(1, devices, lambda k: copy(k).start())

        def finish():
            def arrival(k):
                source = lax.rem(me + k, devices)
                here = by_device.at[slot, source]
                remote(here, here, sum_send.at[k], sum_recv.at[slot, source], peer(k)).wait_recv()

            each(1, devices, arrival)
            each(1, devices, lambda k: copy(k).wait_send())
            if devices <= 32:
                parts = [by_device[slot, k] for k in range(devices)]
                while len(parts) > 1:
                    parts = [a + b for a, b in zip(parts[::2], parts[1::2])] + parts[len(parts) // 2 * 2 :]
                total = parts[0]
            else:
                total = lax.fori_loop(1, devices, lambda k, t: t + by_device[slot, k], by_device[slot, 0])
            return [total[:, k : k + 1] for k in range(DOTS)]

        return finish

    def wide(scalar):
        return jnp.broadcast_to(scalar, (rows, LANES))

    def added(sums, pairs):
        return tuple(total + a * b for total, (a, b) in zip(sums, pairs))

    def stencil_into(dst, edges):
        def emit(c, v, image):
            dst[:, c] = image
            if edges:
                keep_edges(c, image)

        return emit

    def exchange(slot):
        halos = halo_copies(slot)
        start(halos)
        return halos

    def arrive(halos):
        wait_recv(halos)
        wait_send(halos)

    first, coefs = exchange(1), coef_copies()
    start(coefs)
    arrive(first)
    arrive(coefs)
    none = jnp.zeros((rows, LANES), jnp.float32)
    opening = [(none,) * 3]

    def begin(c, v, image):
        r1[:, c] = image
        keep_edges(c, image)
        opening[0] = added(opening[0], ((v, v), (v, image), (image, image)))

    stencil(r0, 1, begin)

    def block(i, state, last=False):
        sums, gamma_old, alpha_old = state
        slot = lax.rem(i, 2)
        arrive(exchange(0))
        cross = [(none,)]

        def second(c, v, image):
            r2[:, c] = image
            if not last:
                keep_edges(c, image)
            cross[0] = added(cross[0], ((v, image),))

        stencil(r1, 0, second)
        if not last:
            halos = exchange(1)
        finish = reduce(slot, sums + cross[0])
        if not last:
            arrive(halos)
            stencil(r2, 1, stencil_into(r3, False))
        r0r0, r0r1, r1r1, r0q1, q0q1, r1q1, q1q1, r1q2, q1q2, r1r2 = finish()
        beta = jnp.where(i == 0, jnp.zeros_like(r0r0), r0r0 / gamma_old)
        pap = r0r1 + beta * (2.0 * r0q1 + beta * q0q1)
        r0p1 = r0r1 + beta * r0q1
        p1p1 = r1r1 + beta * (2.0 * r1q1 + beta * q1q1)
        r1p1 = r1r1 + beta * r1q1
        p1p2 = r1r2 + beta * (2.0 * r1q2 + beta * q1q2)
        alpha = r0r0 / pap
        gamma = r0r0 - alpha * (2.0 * r0p1 - alpha * p1p1)
        beta_next = gamma / r0r0
        m0p1 = r0p1 - alpha * p1p1
        m0m1 = r0r1 - alpha * (2.0 * r1p1 - alpha * p1p2)
        alpha_next = gamma / (m0m1 + beta_next * (2.0 * m0p1 + beta_next * pap))
        b, a, b_, a_ = wide(beta), wide(alpha), wide(beta_next), wide(alpha_next)
        inverse = wide(1.0 / alpha_old)
        sums = (none,) * (DOTS - 1)
        for j in range(tiles):
            c = at(j)
            v0, v1, v2 = r0[:, c], r1[:, c], r2[:, c]
            p0 = v0 + b * q0[:, c]
            p1 = v1 + b * q1[:, c]
            p2 = v2 + b * q2[:, c]
            m0 = v0 - a * p1
            m1 = v1 - a * p2
            d0 = m0 + b_ * p0
            d1 = m1 + b_ * p1
            x[:, c] = x[:, c] + (a * p0 + a_ * d0)
            f0 = m0 - a_ * d1
            r0[:, c] = f0
            if not last:
                p3 = r3[:, c] + b * (inverse * (old2[:, c] - v2))
                m2 = v2 - a * p3
                d2 = m2 + b_ * p2
                f1 = m1 - a_ * d2
                r1[:, c] = f1
                q0[:, c] = d0
                q1[:, c] = d1
                q2[:, c] = d2
                old2[:, c] = m2
                keep_edges(c, f1)
                sums = added(
                    sums,
                    ((f0, f0), (f0, f1), (f1, f1), (f0, d1), (d0, d1), (f1, d1), (d1, d1), (f1, d2), (d1, d2)),
                )
        return sums, gamma, alpha_next

    unity = jnp.ones((1, 1), jnp.float32)
    state = (opening[0] + (none,) * (DOTS - 4), unity, unity)
    state = lax.fori_loop(0, ITERS // 2 - 1, block, state)
    block(ITERS // 2 - 1, state, last=True)


def solution(mesh):
    nr, nc = mesh.shape["rows"], mesh.shape["cols"]

    def on_device(*inputs):
        rows, cols = inputs[0].shape
        block = jax.ShapeDtypeStruct((rows, cols), jnp.float32)

        def held(*shape):
            return pltpu.VMEM(shape, jnp.float32)

        dma = pltpu.SemaphoreType.DMA
        return pl.pallas_call(
            functools.partial(kernel, nr, nc),
            out_shape=(block, block),
            in_specs=[pl.BlockSpec(memory_space=pltpu.VMEM)] * 5,
            out_specs=[pl.BlockSpec(memory_space=pltpu.VMEM)] * 2,
            scratch_shapes=[held(rows, cols)] * 10
            + [held(rows, LANES), held(1, cols), held(rows, LANES), held(1, cols)]
            + [held(2, rows, LANES), held(2, rows, LANES), held(2, 1, cols), held(2, 1, cols)]
            + [held(rows, LANES), held(rows, LANES), held(1, cols), held(1, cols)]
            + [held(DOTS, LANES), held(2, nr * nc, 1, LANES)]
            + [dma((2,)), dma((2,)), dma((4,)), dma((2, 4)), dma((nr * nc,)), dma((2, nr * nc))],
            compiler_params=pltpu.CompilerParams(collective_id=0, has_side_effects=True),
        )(*inputs)

    spec = P("rows", "cols")
    return jax.shard_map(
        on_device, mesh=mesh, in_specs=(spec,) * 5, out_specs=(spec, spec), check_vma=False
    )
```

```python
import functools

import jax
import jax.numpy as jnp
from jax import lax
from jax.experimental import pallas as pl
from jax.experimental.pallas import tpu as pltpu
from jax.sharding import PartitionSpec as P

ITERS = 12

prior_weight = 0.1
smooth_weight = 2.0
LANES = 128
DOTS = 10
MESH = pl.DeviceIdType.MESH


def each(start, stop, body):
    if stop - start < 32:
        for k in range(start, stop):
            body(k)
    else:
        lax.fori_loop(start, stop, lambda k, c: (body(k), c)[1], 0)


def kernel(
    nr, nc,
    depth, hit_mask, hit_count, grad_h, grad_v,
    x, r0,
    conf, east, south, r1, r2, r3, q0, q1, q2, old2,
    e_left, s_above, e_send, s_send,
    left, right, above, below, first_tile, last_tile, top, bottom,
    folds, by_device,
    coef_send, coef_recv, halo_send, halo_recv, sum_send, sum_recv,
):
    me_r = lax.axis_index("rows")
    me_c = lax.axis_index("cols")
    rows, cols = depth.shape
    tiles = cols // LANES
    has_above, has_below = me_r > 0, me_r < nr - 1
    has_left, has_right = me_c > 0, me_c < nc - 1

    devices = nr * nc
    me = me_r * nc + me_c

    def peer(k):
        other = lax.rem(me + k, devices)
        return (other // nc, lax.rem(other, nc))

    barrier = pltpu.get_barrier_semaphore()
    each(1, devices, lambda k: pl.semaphore_signal(barrier, inc=1, device_id=peer(k), device_id_type=MESH))

    row_id = lax.broadcasted_iota(jnp.int32, (rows, LANES), 0)
    lane_id = lax.broadcasted_iota(jnp.int32, (rows, LANES), 1)

    def at(j):
        return slice(j * LANES, (j + 1) * LANES)

    for j in range(tiles):
        c = at(j)
        confidence = (hit_mask[:, c] * hit_count[:, c]).astype(jnp.float32) + prior_weight
        h, v = grad_h[:, c], grad_v[:, c]
        e = smooth_weight * jnp.exp(-0.5 * h * h)
        if j == tiles - 1:
            e = jnp.where(jnp.logical_and(lane_id == LANES - 1, jnp.logical_not(has_right)), 0.0, e)
        so = smooth_weight * jnp.exp(-0.5 * v * v)
        so = jnp.where(jnp.logical_and(row_id == rows - 1, jnp.logical_not(has_below)), 0.0, so)
        b = confidence * depth[:, c]
        zero = jnp.zeros((rows, LANES), jnp.float32)
        conf[:, c] = confidence
        east[:, c] = e
        south[:, c] = so
        r0[:, c] = b
        for held in (x, q0, q1, q2, old2):
            held[:, c] = zero
        s_send[:, c] = so[rows - 1 :, :]
        top[:, c] = b[:1, :]
        bottom[:, c] = b[rows - 1 :, :]
        if j == 0:
            first_tile[...] = b
        if j == tiles - 1:
            last_tile[...] = b
            e_send[...] = e

    @pl.when(jnp.logical_not(has_above))
    def _():
        s_above[...] = jnp.zeros_like(s_above)
        above[...] = jnp.zeros_like(above)

    @pl.when(jnp.logical_not(has_below))
    def _():
        below[...] = jnp.zeros_like(below)

    @pl.when(jnp.logical_not(has_left))
    def _():
        e_left[...] = jnp.zeros_like(e_left)
        left[...] = jnp.zeros_like(left)

    @pl.when(jnp.logical_not(has_right))
    def _():
        right[...] = jnp.zeros_like(right)

    pl.semaphore_wait(barrier, devices - 1)

    up, down = (me_r - 1, me_c), (me_r + 1, me_c)
    lefthand, righthand = (me_r, me_c - 1), (me_r, me_c + 1)

    def remote(src, dst, send, recv, to):
        return pltpu.make_async_remote_copy(
            src_ref=src, dst_ref=dst, send_sem=send, recv_sem=recv, device_id=to, device_id_type=MESH
        )

    def halo_copies(slot):
        return (
            (remote(top, below.at[slot], halo_send.at[0], halo_recv.at[slot, 0], up), has_above, has_below),
            (remote(bottom, above.at[slot], halo_send.at[1], halo_recv.at[slot, 1], down), has_below, has_above),
            (remote(first_tile, right.at[slot], halo_send.at[2], halo_recv.at[slot, 2], lefthand), has_left, has_right),
            (remote(last_tile, left.at[slot], halo_send.at[3], halo_recv.at[slot, 3], righthand), has_right, has_left),
        )

    def coef_copies():
        return (
            (remote(s_send, s_above, coef_send.at[0], coef_recv.at[0], down), has_below, has_above),
            (remote(e_send, e_left, coef_send.at[1], coef_recv.at[1], righthand), has_right, has_left),
        )

    def start(copies):
        for copy, sends, _ in copies:
            pl.when(sends)(copy.start)

    def wait_recv(copies):
        for copy, _, receives in copies:
            pl.when(receives)(copy.wait_recv)

    def wait_send(copies):
        for copy, sends, _ in copies:
            pl.when(sends)(copy.wait_send)

    def to_left(v):
        return pltpu.roll(v, LANES - 1, 1)

    def to_right(v):
        return pltpu.roll(v, 1, 1)

    def stencil(src, dst):
        v = src[:, at(0)]
        moved, carried = to_left(v), jnp.zeros((rows, LANES), jnp.float32)
        for j in range(tiles):
            c = at(j)
            final = j + 1 == tiles
            following = v if final else src[:, at(j + 1)]
            moved_next = v if final else to_left(following)
            flow = east[:, c] * (v - jnp.where(lane_id < LANES - 1, moved, moved_next))
            if final:
                flow = jnp.where(lane_id < LANES - 1, flow, 0.0)
            shifted = to_right(flow)
            from_left = jnp.where(lane_id > 0, shifted, carried)
            fall = jnp.where(row_id < rows - 1, south[:, c] * (v - pltpu.roll(v, rows - 1, 0)), 0.0)
            dst[:, c] = conf[:, c] * v + ((flow - from_left) + (fall - pltpu.roll(fall, 1, 0)))
            v, moved, carried = following, moved_next, shifted

    def finish_edges(src, dst, slot):
        v = src[:, at(0)]
        near = to_left(v)
        flow = to_right(e_left[...] * (left[slot] - near))
        dst[:, at(0)] = dst[:, at(0)] - jnp.where(lane_id == 0, flow, 0.0)
        c = at(tiles - 1)
        v = src[:, c]
        flow = east[:, c] * (v - to_left(right[slot]))
        dst[:, c] = dst[:, c] + jnp.where(lane_id == LANES - 1, flow, 0.0)
        upper = s_above[...] * (above[slot] - src[0:1, :])
        dst[0:1, :] = dst[0:1, :] - upper
        lower = south[rows - 1 :, :] * (src[rows - 1 :, :] - below[slot])
        dst[rows - 1 :, :] = dst[rows - 1 :, :] + lower

    def keep_all_edges(value):
        top[...] = value[:1, :]
        bottom[...] = value[rows - 1 :, :]
        first_tile[...] = value[:, at(0)]
        last_tile[...] = value[:, at(tiles - 1)]

    def dots(pairs):
        sums = [jnp.zeros((rows, LANES), jnp.float32)] * len(pairs)
        for j in range(tiles):
            c = at(j)
            sums = [total + a[:, c] * b[:, c] for total, (a, b) in zip(sums, pairs)]
        return tuple(sums)

    def folded(acc):
        return jnp.sum(acc, axis=0, keepdims=True)

    def folded(acc):
        return jnp.sum(acc, axis=0, keepdims=True)

    def keep_edges(c, value):
        top[:, c] = value[:1, :]
        bottom[:, c] = value[rows - 1 :, :]
        if c.start == 0:
            first_tile[...] = value
        if c.stop == cols:
            last_tile[...] = value

    def reduce(slot, sums):
        for k in range(DOTS):
            folds[k : k + 1, :] = folded(sums[k])
        part = jnp.broadcast_to(jnp.sum(folds[...], axis=1, keepdims=True), (DOTS, LANES))
        mine = lax.broadcasted_iota(jnp.int32, (DOTS, LANES), 0) == lax.broadcasted_iota(jnp.int32, (DOTS, LANES), 1)
        by_device[slot, me] = folded(jnp.where(mine, part, 0.0))

        def copy(k):
            here = by_device.at[slot, me]
            return remote(here, here, sum_send.at[k], sum_recv.at[slot, me], peer(k))

        each(1, devices, lambda k: copy(k).start())

        def finish():
            def arrival(k):
                source = lax.rem(me + k, devices)
                here = by_device.at[slot, source]
                remote(here, here, sum_send.at[k], sum_recv.at[slot, source], peer(k)).wait_recv()

            each(1, devices, arrival)
            each(1, devices, lambda k: copy(k).wait_send())
            if devices <= 32:
                parts = [by_device[slot, k] for k in range(devices)]
                while len(parts) > 1:
                    parts = [a + b for a, b in zip(parts[::2], parts[1::2])] + parts[len(parts) // 2 * 2 :]
                total = parts[0]
            else:
                total = lax.fori_loop(1, devices, lambda k, t: t + by_device[slot, k], by_device[slot, 0])
            return [total[:, k : k + 1] for k in range(DOTS)]

        return finish

    def wide(scalar):
        return jnp.broadcast_to(scalar, (rows, LANES))

    def added(sums, pairs):
        return tuple(total + a * b for total, (a, b) in zip(sums, pairs))

    def exchange(slot):
        halos = halo_copies(slot)
        start(halos)
        return halos

    def arrive(halos):
        wait_recv(halos)
        wait_send(halos)

    first, coefs = exchange(1), coef_copies()
    start(coefs)
    stencil(r0, r1)
    arrive(first)
    arrive(coefs)
    finish_edges(r0, r1, 1)
    keep_all_edges(r1)
    none = jnp.zeros((rows, LANES), jnp.float32)
    opening = dots(((r0, r0), (r0, r1), (r1, r1)))

    def block(i, state, last=False):
        sums, gamma_old, alpha_old = state
        slot = lax.rem(i, 2)
        halos = exchange(0)
        stencil(r1, r2)
        arrive(halos)
        finish_edges(r1, r2, 0)
        if not last:
            keep_all_edges(r2)
            halos = exchange(1)
        finish = reduce(slot, sums + dots(((r1, r2),)))
        if not last:
            stencil(r2, r3)
            arrive(halos)
            finish_edges(r2, r3, 1)
        r0r0, r0r1, r1r1, r0q1, q0q1, r1q1, q1q1, r1q2, q1q2, r1r2 = finish()
        beta = jnp.where(i == 0, jnp.zeros_like(r0r0), r0r0 / gamma_old)
        pap = r0r1 + beta * (2.0 * r0q1 + beta * q0q1)
        r0p1 = r0r1 + beta * r0q1
        p1p1 = r1r1 + beta * (2.0 * r1q1 + beta * q1q1)
        r1p1 = r1r1 + beta * r1q1
        p1p2 = r1r2 + beta * (2.0 * r1q2 + beta * q1q2)
        alpha = r0r0 / pap
        gamma = r0r0 - alpha * (2.0 * r0p1 - alpha * p1p1)
        beta_next = gamma / r0r0
        m0p1 = r0p1 - alpha * p1p1
        m0m1 = r0r1 - alpha * (2.0 * r1p1 - alpha * p1p2)
        alpha_next = gamma / (m0m1 + beta_next * (2.0 * m0p1 + beta_next * pap))
        b, a, b_, a_ = wide(beta), wide(alpha), wide(beta_next), wide(alpha_next)
        inverse = wide(1.0 / alpha_old)
        sums = (none,) * (DOTS - 1)
        for j in range(tiles):
            c = at(j)
            v0, v1, v2 = r0[:, c], r1[:, c], r2[:, c]
            p0 = v0 + b * q0[:, c]
            p1 = v1 + b * q1[:, c]
            p2 = v2 + b * q2[:, c]
            m0 = v0 - a * p1
            m1 = v1 - a * p2
            d0 = m0 + b_ * p0
            d1 = m1 + b_ * p1
            x[:, c] = x[:, c] + (a * p0 + a_ * d0)
            f0 = m0 - a_ * d1
            r0[:, c] = f0
            if not last:
                p3 = r3[:, c] + b * (inverse * (old2[:, c] - v2))
                m2 = v2 - a * p3
                d2 = m2 + b_ * p2
                f1 = m1 - a_ * d2
                r1[:, c] = f1
                q0[:, c] = d0
                q1[:, c] = d1
                q2[:, c] = d2
                old2[:, c] = m2
                keep_edges(c, f1)
                sums = added(
                    sums,
                    ((f0, f0), (f0, f1), (f1, f1), (f0, d1), (d0, d1), (f1, d1), (d1, d1), (f1, d2), (d1, d2)),
                )
        return sums, gamma, alpha_next

    unity = jnp.ones((1, 1), jnp.float32)
    state = (opening + (none,) * (DOTS - 4), unity, unity)
    state = lax.fori_loop(0, ITERS // 2 - 1, block, state)
    block(ITERS // 2 - 1, state, last=True)


def solution(mesh):
    nr, nc = mesh.shape["rows"], mesh.shape["cols"]

    def on_device(*inputs):
        rows, cols = inputs[0].shape
        block = jax.ShapeDtypeStruct((rows, cols), jnp.float32)

        def held(*shape):
            return pltpu.VMEM(shape, jnp.float32)

        dma = pltpu.SemaphoreType.DMA
        return pl.pallas_call(
            functools.partial(kernel, nr, nc),
            out_shape=(block, block),
            in_specs=[pl.BlockSpec(memory_space=pltpu.VMEM)] * 5,
            out_specs=[pl.BlockSpec(memory_space=pltpu.VMEM)] * 2,
            scratch_shapes=[held(rows, cols)] * 10
            + [held(rows, LANES), held(1, cols), held(rows, LANES), held(1, cols)]
            + [held(2, rows, LANES), held(2, rows, LANES), held(2, 1, cols), held(2, 1, cols)]
            + [held(rows, LANES), held(rows, LANES), held(1, cols), held(1, cols)]
            + [held(DOTS, LANES), held(2, nr * nc, 1, LANES)]
            + [dma((2,)), dma((2,)), dma((4,)), dma((2, 4)), dma((nr * nc,)), dma((2, nr * nc))],
            compiler_params=pltpu.CompilerParams(collective_id=0, has_side_effects=True),
        )(*inputs)

    spec = P("rows", "cols")
    return jax.shard_map(
        on_device, mesh=mesh, in_specs=(spec,) * 5, out_specs=(spec, spec), check_vma=False
    )
```
